512 devices in a mesh: grp: 16 (over z_lo, core), row: 32 (over x, y, z_hi).
Axes of the slice: x: 4, y: 4, z: 16 (z_hi: 2, z_lo: 8; z = z_hi * 8 + z_lo), core: 2. Of those that a mesh axis runs over, the one named last changes fastest.
Arguments:
- signal: bfloat16 [2048, 64, 128], P(('grp', 'row')), may hold values from -6 to 6
- leaf_basis: bfloat16 [2048, 64, 128], P(('grp', 'row')), may hold values from -0.5 to 0.5
- near_blocks: bfloat16 [2048, 3, 128, 128], P(('grp', 'row')), may hold values from -0.3125 to 0.3125
- coupling: bfloat16 [98304, 4096], P(('grp', 'row')), may hold values from -0.109375 to 0.109375
- block_cols: int32 [98304], P(('grp', 'row')), may hold values from 0 to 2047, as said below
- block_rows: int32 [98304], P(('grp', 'row')), may hold values from 0 to 3
- block_live: int32 [98304], P(('grp', 'row')), may hold values 0 or 1
Outputs:
- product: bfloat16 [2048, 64, 128], P(('grp', 'row'))
The draws below stay inside these ranges and needn't reach their ends.
Inputs may be any that keep to these rules, and one draw needn't show every extreme that they name: `block_cols`: slot b of device d (d = b // 192, in group h = d // 32) names a column cluster of group (h + o) mod (16), where o = (b mod 192) // 64 - 1; a group's clusters are g * 128 to (g + 1) * 128 - 1.
All inputs are finite; a program needn't handle non-finite values. No bound on the sum of `block_live` on one device may be relied on, other than what follows from the above.
Results may differ from the reference program's by a relative error of at most 0.0039.
Values may be sent and summed in bfloat16 or wider, within the bound.
A program may use at most 64 MiB of HBM per device.

```python
import jax
import jax.numpy as jnp
from jax import lax

LEAF = 128
K = 64
R = 64
CL_DEV = 4
BPC = 16
BPG = 64
NBLK_DEV = 192
GC = 128
CLUST = 2048
BLOCKS = 98304
DEVICES = 512


def draw_block_cols(key, part):
    slot_ids = jnp.arange(BLOCKS, dtype=jnp.int32)
    device = slot_ids // NBLK_DEV
    offset = slot_ids % NBLK_DEV // BPG - 1
    home_group = device * CL_DEV // GC
    group_count = CLUST // GC
    column_group = (home_group + offset + group_count) % group_count
    within = jax.random.randint(key, (BLOCKS,), 0, GC, dtype=jnp.int32)
    return column_group * GC + within


def plant(values, own_key, low, top_value):
    longest = values.shape.index(max(values.shape))
    spots = []
    for shift in (0, 1):
        where = [jax.random.randint(jax.random.fold_in(own_key, axis), (), 0, length) for axis, length in enumerate(values.shape)]
        where[longest] = (where[longest] + shift) % values.shape[longest]
        spots.append(tuple(where))
    return values.at[spots[0]].set(low).at[spots[1]].set(top_value)


def level_of(key, shape, shards, least, high):
    level = 1.0
    for position, parts in shards:
        steps = jax.random.uniform(jax.random.fold_in(jax.random.fold_in(key, 6), position), (parts,), jnp.float32, least / len(shards), high / len(shards))
        level = level * jnp.repeat(jnp.exp(steps), shape[position] // parts).reshape((-1,) + (1,) * (len(shape) - 1 - position))
    return level


def bell_draw(key, shape, width, bound, split=(), kind=jnp.bfloat16):
    array = width * jax.random.normal(key, shape, jnp.float32)
    if split:
        array = array * level_of(key, shape, split, -0.22, 0.18)
    return jnp.clip(array, -bound, bound).astype(kind)


def setup_inputs(seed: int = 0) -> dict:
    key_of = jax.random.split(jax.random.key(seed), 8)
    signal = bell_draw(key_of[0], (CLUST, R, LEAF), 1.0, 6.0, ((0, 512),))
    leaf_basis = bell_draw(key_of[1], (CLUST, K, LEAF), LEAF ** -0.5, 0.5, ((0, 512),))
    near_blocks = bell_draw(key_of[2], (CLUST, 3, LEAF, LEAF), (3 * LEAF) ** -0.5, 0.3125, ((0, 512),))
    coupling = bell_draw(key_of[3], (BLOCKS, K * K), (3 * BPC * K) ** -0.5, 0.109375, ((0, 512),))
    block_cols = draw_block_cols(jax.random.fold_in(key_of[7], 71), 0)
    block_rows = plant(jax.random.randint(key_of[5], (BLOCKS,), 0, CL_DEV), jax.random.fold_in(key_of[5], 1), 0, CL_DEV - 1).astype(jnp.int32)
    block_live = plant((jax.random.randint(key_of[6], (BLOCKS,), 0, 4) < 3).astype(jnp.int32), jax.random.fold_in(key_of[6], 1), 0, 1)
    return dict(signal=signal, leaf_basis=leaf_basis, near_blocks=near_blocks, coupling=coupling, block_cols=block_cols, block_rows=block_rows, block_live=block_live)


def reference(signal, leaf_basis, near_blocks, coupling, block_cols, block_rows, block_live):
    skeleton = jnp.einsum('crl,ckl->crk', signal.astype(jnp.float32), leaf_basis.astype(jnp.float32)).astype(jnp.bfloat16)
    blocks_all = coupling.reshape(DEVICES, NBLK_DEV, K, K)
    columns = block_cols.reshape(DEVICES, NBLK_DEV)
    row_ids = block_rows.reshape(DEVICES, NBLK_DEV)
    live_mask = block_live.reshape(DEVICES, NBLK_DEV)
    cluster_ids = jnp.arange(CL_DEV, dtype=jnp.int32)

    def device_far(pieces):
        blocks, cols_here, rows_here, live_here = pieces
        sources = skeleton[cols_here].astype(jnp.float32)
        contrib = jnp.einsum('brm,bkm->brk', sources, blocks.astype(jnp.float32))
        contrib = contrib * live_here.astype(jnp.float32)[:, None, None]
        one_hot = (rows_here[None, :] == cluster_ids[:, None]).astype(jnp.float32)
        return jnp.einsum('cb,brk->crk', one_hot, contrib, precision=lax.Precision.HIGHEST)

    far = lax.map(device_far, (blocks_all, columns, row_ids, live_mask)).reshape(CLUST, R, K)
    far_skeleton = far.astype(jnp.bfloat16)
    total = jnp.einsum('crk,ckl->crl', far_skeleton.astype(jnp.float32), leaf_basis.astype(jnp.float32))
    zero_cluster = jnp.zeros((1, R, LEAF), jnp.bfloat16)
    before = jnp.concatenate([zero_cluster, signal[:-1]], axis=0)
    after = jnp.concatenate([signal[1:], zero_cluster], axis=0)
    for index, neighbour in enumerate([before, signal, after]):
        total = total + jnp.einsum('crl,cml->crm', neighbour.astype(jnp.float32), near_blocks[:, index].astype(jnp.float32))
    return total.astype(jnp.bfloat16)
```

```python
import functools

import jax
import jax.numpy as jnp
from jax import lax
from jax.experimental import pallas as pl
from jax.experimental.pallas import tpu as pltpu
from jax.sharding import PartitionSpec as P

MESH = pl.DeviceIdType.MESH
F32 = jnp.float32
BF16 = jnp.bfloat16

CL = 4
R = 64
LEAF = 128
GSLOTS = 64
HALF = 32
LANES = 128
SIDE = 4


def one_hot(rows, columns, chosen):
    row = lax.broadcasted_iota(jnp.int32, (rows, columns), 0)
    column = lax.broadcasted_iota(jnp.int32, (rows, columns), 1)
    return jnp.where(column == chosen(row), 1.0, 0.0).astype(BF16)


def nt(a, b):
    return lax.dot_general(a, b, (((1,), (1,)), ((), ())), preferred_element_type=F32)


def nn(a, b):
    return jnp.dot(a, b, preferred_element_type=F32)


def kernel(
    nx, ny, nz,
    cols_ref, rows_ref, live_ref, sig_hbm, leaf_hbm, near_hbm, coup_hbm, out_ref,
    sig, leaf, near, coup, own, sibling, neighbour, halo,
    lhs, gathered, acc, total, perm1, perm2, leaf_perm,
    local_sem, send_sem, recv_sem,
):
    grp = lax.axis_index("grp")
    row = lax.axis_index("row")
    n_grp, n_row = 2 * nz, 2 * nx * ny
    z, core = grp // 2, grp % 2
    xy, plane = row // 2, row % 2
    x, y = xy // ny, xy % ny

    def device(x_, y_, plane_):
        return (grp, (x_ * ny + y_) * 2 + plane_)

    opposite = device(x, y, 1 - plane)
    sib = (z * 2 + 1 - core, row)
    step = 2 * core - 1
    z_full = (plane * nz + z + step + 2 * nz) % (2 * nz)
    next_plane = z_full // nz
    near_z = ((z_full % nz) * 2 + 1 - core, xy * 2 + next_plane)
    x_peers = [((x + d) % nx, device((x + d) % nx, y, plane)) for d in range(1, nx)]
    y_peers = [((y + d) % ny, device(x, (y + d) % ny, plane)) for d in range(1, ny)]
    linear = grp * n_row + row
    count = n_grp * n_row
    after, before = (linear + 1) % count, (linear + count - 1) % count
    after_dev = (after // n_row, after % n_row)
    before_dev = (before // n_row, before % n_row)

    mine = pl.ds(plane * CL, CL)
    other_start = (1 - plane) * CL
    next_mine = pl.ds(next_plane * CL, CL)

    stage = []
    for i, (src, dst) in enumerate(((leaf_hbm, leaf), (sig_hbm, sig), (coup_hbm, coup), (near_hbm, near))):
        stage.append(pltpu.make_async_copy(src, dst, local_sem.at[i]))
        stage[-1].start()

    barrier = pltpu.get_barrier_semaphore()
    friends = [opposite, sib, near_z, after_dev, before_dev]
    friends += [dev for _, dev in x_peers] + [dev for _, dev in y_peers]
    for friend in friends:
        pl.semaphore_signal(barrier, inc=1, device_id=friend, device_id_type=MESH)

    stage[0].wait()
    stage[1].wait()
    zero = jnp.zeros((R, LEAF), BF16)
    for c in range(CL):
        a = jnp.concatenate([leaf[c, 0:HALF], leaf[c, HALF : 2 * HALF]], axis=1)
        s = sig[c]
        b = jnp.concatenate(
            [jnp.concatenate([s, zero], axis=1), jnp.concatenate([zero, s], axis=1)], axis=0
        )
        own[x, y, plane * CL + c] = nt(a, b).astype(BF16)

    pl.semaphore_wait(barrier, len(friends))

    slots = [0]

    def send(src, dst, dev):
        i = slots[0]
        slots[0] += 1
        copy = pltpu.make_async_remote_copy(
            src_ref=src, dst_ref=dst, send_sem=send_sem.at[i], recv_sem=recv_sem.at[i],
            device_id=dev, device_id_type=MESH,
        )
        copy.start()
        return copy

    everything = []

    def send_all(items):
        copies = [send(*item) for item in items]
        everything.extend(copies)
        return copies

    def arrived(copies):
        for copy in copies:
            copy.wait_recv()

    block = own.at[x, y, mine]
    z_far, = send_all([(block, block, opposite)])
    z_near, = send_all([(block, neighbour.at[x, y, mine], near_z)])
    a1 = send_all([(block, block, dev) for _, dev in x_peers])
    h_after, = send_all([(sig.at[CL - 1], halo.at[0], after_dev)])
    h_before, = send_all([(sig.at[0], halo.at[1], before_dev)])

    t_count, a_count, j_count = 16, 4, 32
    size = t_count * j_count
    perm1[...] = one_hot(size, size, lambda r: (r % j_count) * t_count + r // j_count)

    def column_of(c):
        kp, h, rest = c // 256, (c // 128) % 2, c % 128
        return (rest // HALF) * 128 + kp * 64 + h * HALF + rest % HALF

    r_i = lax.broadcasted_iota(jnp.int32, (size, size), 0)
    c_i = lax.broadcasted_iota(jnp.int32, (size, size), 1)
    perm2[...] = jnp.where(r_i == column_of(c_i), 1.0, 0.0).astype(BF16)
    reorder = one_hot(R, R, lambda r: (r % HALF) * 2 + r // HALF)
    for c in range(CL):
        leaf_perm[c] = nn(reorder, leaf[c]).astype(BF16)

    places = (1, jnp.where(core == 0, 2, 0), jnp.where(core == 0, 0, 2))

    def prepare(s):
        first = pl.multiple_of(places[s] * GSLOTS, GSLOTS)
        x_rows = []
        for j in range(j_count):
            x_rows.append(jnp.concatenate(
                [coup[pl.ds(first + a * t_count, t_count), j * LANES : (j + 1) * LANES]
                 for a in range(a_count)], axis=1))
        xs = jnp.concatenate(x_rows, axis=0)
        ys = nn(perm1[...], xs).astype(BF16)
        ws = nn(ys, perm2[...]).astype(BF16)
        lane_slot = lax.broadcasted_iota(jnp.int32, (1, LANES), 1) // HALF
        for t in range(t_count):
            code = jnp.full((1, LANES), -1, jnp.int32)
            for a in range(a_count):
                b = first + a * t_count + t
                here = jnp.where(live_ref[b] != 0, rows_ref[b], -1)
                code = jnp.where(lane_slot == a, here, code)
            for i in range(CL):
                mask = jnp.where(code == i, 1.0, 0.0)
                mask = jnp.broadcast_to(mask, (j_count, LANES)).astype(BF16)
                for kp in range(2):
                    for h in range(2):
                        tile = ws[t * j_count : (t + 1) * j_count,
                                  (kp * 2 + h) * LANES : (kp * 2 + h + 1) * LANES]
                        lhs[s, (h * CL + i) * R + kp * HALF : (h * CL + i) * R + (kp + 1) * HALF,
                            t * LANES : (t + 1) * LANES] = tile * mask

    def multiply(s, panel):
        first = places[s] * GSLOTS
        for t in range(t_count):
            for a in range(a_count):
                c = lax.rem(cols_ref[first + a * t_count + t], n_row * CL)
                at = (t * a_count + a) * HALF
                gathered[at : at + HALF] = panel[c // (8 * ny), (c // 8) % ny, c % 8]
        part = nn(lhs[s], gathered[...])
        if s == 0:
            acc[...] = part
        else:
            acc[...] += part

    stage[2].wait()
    prepare(0)

    z_near.wait_recv()
    n_block = neighbour.at[x, y, next_mine]
    n1 = send_all([(n_block, n_block, dev) for _, dev in y_peers])
    arrived(a1)
    a_column = own.at[:, y, mine]
    a2 = send_all([(a_column, a_column, dev) for _, dev in y_peers])

    z_far.wait_recv()
    lower, upper = pl.ds(other_start, 2), pl.ds(other_start + 2, 2)
    b1y = send_all([(own.at[x, y, lower], own.at[x, y, lower], dev) for _, dev in y_peers])
    b1x = send_all([(own.at[x, y, upper], own.at[x, y, upper], dev) for _, dev in x_peers])
    prepare(1)

    arrived(n1)
    n_row_ref = neighbour.at[x, :, next_mine]
    n2 = send_all([(n_row_ref, n_row_ref, dev) for _, dev in x_peers])
    arrived(b1y)
    b_row = own.at[x, :, lower]
    b2x = send_all([(b_row, b_row, dev) for _, dev in x_peers])
    fwd = send_all([(b_row, neighbour.at[x, :, lower], near_z)])
    arrived(b1x)
    b_col = own.at[:, y, upper]
    b2y = send_all([(b_col, b_col, dev) for _, dev in y_peers])
    fwd += send_all([(b_col, neighbour.at[:, y, upper], near_z)])
    prepare(2)

    arrived(a2)
    s_all = send_all([(own.at[:, :, mine], sibling.at[:, :, mine], sib)])
    for (px, _), copy in zip(x_peers, b2x):
        from_x = (x + nx - (px - x)) % nx
        copy.wait_recv()
        fwd += send_all([(own.at[from_x, :, lower], neighbour.at[from_x, :, lower], near_z)])
    for (py, _), copy in zip(y_peers, b2y):
        from_y = (y + ny - (py - y)) % ny
        copy.wait_recv()
        fwd += send_all([(own.at[:, from_y, upper], neighbour.at[:, from_y, upper], near_z)])
    other = pl.ds(other_start, CL)
    s_all += send_all([(own.at[:, :, other], sibling.at[:, :, other], sib)])

    stage[3].wait()
    h_after.wait_recv()
    h_before.wait_recv()
    left = jnp.where(linear == 0, jnp.zeros_like(zero), halo[0])
    right = jnp.where(linear == count - 1, jnp.zeros_like(zero), halo[1])
    signals = [left] + [sig[c] for c in range(CL)] + [right]
    for c in range(CL):
        wide = jnp.concatenate(signals[c : c + 3], axis=1)
        weights = jnp.concatenate([near[c, i] for i in range(3)], axis=1)
        total[c] = nt(wide, weights)

    multiply(0, own)
    arrived(s_all)
    multiply(1, sibling)
    arrived(n2)
    arrived(fwd)
    multiply(2, neighbour)

    both = acc[0 : CL * R] + pltpu.roll(acc[CL * R :], R, 1)
    far = both[:, 0:R].astype(BF16)
    for c in range(CL):
        part = lax.dot_general(
            far[c * R : (c + 1) * R], leaf_perm[c], (((0,), (0,)), ((), ())),
            preferred_element_type=F32,
        )
        out_ref[c] = (total[c] + part).astype(BF16)
    for copy in everything:
        copy.wait_send()


def per_device(nx, ny, nz, signal, leaf_basis, near_blocks, coupling, block_cols, block_rows, block_live):
    smem = pl.BlockSpec(memory_space=pltpu.SMEM)
    hbm = pl.BlockSpec(memory_space=pltpu.HBM)
    panel = pltpu.VMEM((nx, ny, 2 * CL, HALF, LANES), BF16)
    copies = 64
    return pl.pallas_call(
        functools.partial(kernel, nx, ny, nz),
        name="h2_product",
        out_shape=jax.ShapeDtypeStruct((CL, R, LEAF), BF16),
        in_specs=[smem] * 3 + [hbm] * 4,
        out_specs=pl.BlockSpec(memory_space=pltpu.VMEM),
        scratch_shapes=[
            pltpu.VMEM((CL, R, LEAF), BF16),
            pltpu.VMEM((CL, R, LEAF), BF16),
            pltpu.VMEM((CL, 3, LEAF, LEAF), BF16),
            pltpu.VMEM((3 * GSLOTS, R * R), BF16),
            panel, panel, panel,
            pltpu.VMEM((2, R, LEAF), BF16),
            pltpu.VMEM((3, 2 * CL * R, GSLOTS * HALF), BF16),
            pltpu.VMEM((GSLOTS * HALF, LANES), BF16),
            pltpu.VMEM((2 * CL * R, LANES), F32),
            pltpu.VMEM((CL, R, LEAF), F32),
            pltpu.VMEM((512, 512), BF16),
            pltpu.VMEM((512, 512), BF16),
            pltpu.VMEM((CL, R, LEAF), BF16),
            pltpu.SemaphoreType.DMA((4,)),
            pltpu.SemaphoreType.DMA((copies,)),
            pltpu.SemaphoreType.DMA((copies,)),
        ],
        compiler_params=pltpu.CompilerParams(
            collective_id=0, has_side_effects=True, vmem_limit_bytes=48 * 2**20
        ),
    )(block_cols, block_rows, block_live, signal, leaf_basis, near_blocks, coupling)


def solution(mesh, nx=SIDE, ny=SIDE):
    both = ("grp", "row")
    in_specs = (
        P(both, None, None), P(both, None, None), P(both, None, None, None), P(both, None),
        P(both), P(both), P(both),
    )
    nz = mesh.shape["grp"] // 2
    return jax.shard_map(
        functools.partial(per_device, nx, ny, nz), mesh=mesh, in_specs=in_specs,
        out_specs=P(both, None, None), check_vma=False,
    )
```

```python
import functools

import jax
import jax.numpy as jnp
from jax import lax
from jax.experimental import pallas as pl
from jax.experimental.pallas import tpu as pltpu
from jax.sharding import PartitionSpec as P

MESH = pl.DeviceIdType.MESH
F32 = jnp.float32
BF16 = jnp.bfloat16

CL = 4
R = 64
LEAF = 128
GSLOTS = 64
HALF = 32
LANES = 128
SIDE = 4


def one_hot(rows, columns, chosen):
    row = lax.broadcasted_iota(jnp.int32, (rows, columns), 0)
    column = lax.broadcasted_iota(jnp.int32, (rows, columns), 1)
    return jnp.where(column == chosen(row), 1.0, 0.0).astype(BF16)


def ring(n):
    return sorted(range(1, n), key=lambda d: min(d, n - d))


def nt(a, b):
    return lax.dot_general(a, b, (((1,), (1,)), ((), ())), preferred_element_type=F32)


def nn(a, b):
    return jnp.dot(a, b, preferred_element_type=F32)


def kernel(
    nx, ny, nz,
    cols_hbm, rows_hbm, live_hbm, sig_hbm, leaf_hbm, near_hbm, coup_hbm, out_ref,
    cols_ref, rows_ref, live_ref,
    sig, leaf, near, coup, own, sibling, neighbour, halo,
    lhs, gathered, acc, total, perm1, perm2, leaf_perm,
    local_sem, send_sem, recv_sem, hello,
):
    grp = lax.axis_index("grp")
    row = lax.axis_index("row")
    n_grp, n_row = 2 * nz, 2 * nx * ny
    z, core = grp // 2, grp % 2
    xy, plane = row // 2, row % 2
    x, y = xy // ny, xy % ny

    def device(x_, y_, plane_):
        return (grp, (x_ * ny + y_) * 2 + plane_)

    opposite = device(x, y, 1 - plane)
    sib = (z * 2 + 1 - core, row)
    step = 2 * core - 1
    z_here = plane * nz + z
    z_next = (z_here + step + 2 * nz) % (2 * nz)
    next_plane = z_next // nz
    next_grp = (z_next % nz) * 2 + 1 - core
    near_z = (next_grp, xy * 2 + next_plane)
    x_peers = [((x + d) % nx, device((x + d) % nx, y, plane)) for d in ring(nx)]
    y_peers = [((y + d) % ny, device(x, (y + d) % ny, plane)) for d in ring(ny)]
    linear = grp * n_row + row
    count = n_grp * n_row
    after, before = (linear + 1) % count, (linear + count - 1) % count
    edge = jnp.where(plane == 0, before, after)
    edge_dev = (edge // n_row, edge % n_row)

    def key(z_, plane_):
        return jnp.where(plane_ == 0, z_, nz)

    here = key(z, plane)
    k_opp, k_edge = key(z, 1 - plane), key(edge_dev[0] // 2, 1 - plane)
    k_near = key(z_next % nz, next_plane)
    pairs = [
        (dev, here + 1 < there, here > there + 1)
        for dev, there in ((opposite, k_opp), (edge_dev, k_edge), (near_z, k_near))
    ]
    early_opp, early_edge, early_near = [early for _, early, _ in pairs]

    mine = pl.ds(plane * CL, CL)
    other_start = (1 - plane) * CL

    stage = []
    loads = ((leaf_hbm, leaf), (sig_hbm, sig), (coup_hbm, coup), (near_hbm, near),
             (cols_hbm, cols_ref), (rows_hbm, rows_ref), (live_hbm, live_ref))
    for i, (src, dst) in enumerate(loads):
        stage.append(pltpu.make_async_copy(src, dst, local_sem.at[i]))
        stage[-1].start()

    barrier = pltpu.get_barrier_semaphore()

    def greet(semaphore, dev):
        pl.semaphore_signal(semaphore, inc=1, device_id=dev, device_id_type=MESH)

    friends = [sib] + [dev for _, dev in x_peers] + [dev for _, dev in y_peers]
    expected = len(friends)
    for friend in friends:
        greet(barrier, friend)
    for dev, early, late in pairs:
        pl.when(jnp.logical_not(late))(functools.partial(greet, barrier, dev))
        expected = expected + jnp.where(early, 0, 1)

    pl.semaphore_wait(barrier, expected)
    for i, (dev, _, late) in enumerate(pairs):
        pl.when(late)(functools.partial(greet, hello.at[i], dev))

    stage[0].wait()
    stage[1].wait()
    zero = jnp.zeros((R, LEAF), BF16)
    for c in range(CL):
        a = jnp.concatenate([leaf[c, 0:HALF], leaf[c, HALF : 2 * HALF]], axis=1)
        s = sig[c]
        b = jnp.concatenate(
            [jnp.concatenate([s, zero], axis=1), jnp.concatenate([zero, s], axis=1)], axis=0
        )
        own[x, y, plane * CL + c] = nt(a, b).astype(BF16)

    slots = [0]
    everything = []

    def prepared(src, dst, dev):
        i = slots[0]
        slots[0] += 1
        copy = pltpu.make_async_remote_copy(
            src_ref=src, dst_ref=dst, send_sem=send_sem.at[i], recv_sem=recv_sem.at[i],
            device_id=dev, device_id_type=MESH,
        )
        everything.append(copy)
        return copy

    def send_all(items):
        copies = [prepared(*item) for item in items]
        for copy in copies:
            copy.start()
        return copies

    def arrived(copies):
        for copy in copies:
            copy.wait_recv()

    block = own.at[x, y, mine]
    n_dst = neighbour.at[x, y, mine]
    to_opp = prepared(block, block, opposite)
    to_near = prepared(block, n_dst, near_z)
    opp_slot = plane
    halo_opp = prepared(sig.at[(1 - plane) * (CL - 1)], halo.at[opp_slot], opposite)
    halo_edge = prepared(sig.at[plane * (CL - 1)], halo.at[1 - opp_slot], edge_dev)

    def now(early, *copies):
        @pl.when(jnp.logical_not(early))
        def _():
            for copy in copies:
                copy.start()

    def then(i, *copies):
        @pl.when(pairs[i][1])
        def _():
            pl.semaphore_wait(hello.at[i], 1)
            for copy in copies:
                copy.start()

    def spread_first(panel, start):
        low, high = pl.ds(start, 2), pl.ds(start + 2, 2)
        return (
            send_all([(panel.at[x, y, low], panel.at[x, y, low], dev) for _, dev in y_peers]),
            send_all([(panel.at[x, y, high], panel.at[x, y, high], dev) for _, dev in x_peers]),
        )

    def spread_second(panel, start, first):
        low, high = pl.ds(start, 2), pl.ds(start + 2, 2)
        arrived(first[0])
        line = panel.at[x, :, low]
        copies = send_all([(line, line, dev) for _, dev in x_peers])
        arrived(first[1])
        line = panel.at[:, y, high]
        return copies + send_all([(line, line, dev) for _, dev in y_peers])

    now(early_opp, to_opp)
    now(early_near, to_near)
    my_start, next_start = plane * CL, next_plane * CL
    a1 = spread_first(own, my_start)

    t_count, a_count, j_count = 16, 4, 32
    size = t_count * j_count
    perm1[...] = one_hot(size, size, lambda r: (r % j_count) * t_count + r // j_count)

    def column_of(c):
        kp, h, rest = c // 256, (c // 128) % 2, c % 128
        return (rest // HALF) * 128 + kp * 64 + h * HALF + rest % HALF

    r_i = lax.broadcasted_iota(jnp.int32, (size, size), 0)
    c_i = lax.broadcasted_iota(jnp.int32, (size, size), 1)
    perm2[...] = jnp.where(r_i == column_of(c_i), 1.0, 0.0).astype(BF16)
    reorder = one_hot(R, R, lambda r: (r % HALF) * 2 + r // HALF)
    for c in range(CL):
        leaf_perm[c] = nn(reorder, leaf[c]).astype(BF16)

    places = (1, jnp.where(core == 0, 2, 0), jnp.where(core == 0, 0, 2))

    def prepare(s):
        first = pl.multiple_of(places[s] * GSLOTS, GSLOTS)
        x_rows = []
        for j in range(j_count):
            x_rows.append(jnp.concatenate(
                [coup[pl.ds(first + a * t_count, t_count), j * LANES : (j + 1) * LANES]
                 for a in range(a_count)], axis=1))
        xs = jnp.concatenate(x_rows, axis=0)
        ys = nn(perm1[...], xs).astype(BF16)
        ws = nn(ys, perm2[...]).astype(BF16)
        lane_slot = lax.broadcasted_iota(jnp.int32, (1, LANES), 1) // HALF
        for t in range(t_count):
            code = jnp.full((1, LANES), -1, jnp.int32)
            for a in range(a_count):
                b = first + a * t_count + t
                slot_row = jnp.where(live_ref[b] != 0, rows_ref[b], -1)
                code = jnp.where(lane_slot == a, slot_row, code)
            for i in range(CL):
                mask = jnp.where(code == i, 1.0, 0.0)
                mask = jnp.broadcast_to(mask, (j_count, LANES)).astype(BF16)
                for kp in range(2):
                    for h in range(2):
                        tile = ws[t * j_count : (t + 1) * j_count,
                                  (kp * 2 + h) * LANES : (kp * 2 + h + 1) * LANES]
                        lhs[s, (h * CL + i) * R + kp * HALF : (h * CL + i) * R + (kp + 1) * HALF,
                            t * LANES : (t + 1) * LANES] = tile * mask

    def multiply(s, panel):
        first = places[s] * GSLOTS
        for t in range(t_count):
            for a in range(a_count):
                c = lax.rem(cols_ref[first + a * t_count + t], n_row * CL)
                at = (t * a_count + a) * HALF
                gathered[at : at + HALF] = panel[c // (8 * ny), (c // 8) % ny, c % 8]
        part = nn(lhs[s], gathered[...])
        if s == 0:
            acc[...] = part
        else:
            acc[...] += part

    for copy in stage[2:]:
        copy.wait()
    prepare(0)
    a2 = spread_second(own, my_start, a1)
    then(2, to_near)
    to_near.wait_recv()
    n1 = spread_first(neighbour, next_start)
    prepare(1)
    n2 = spread_second(neighbour, next_start, n1)
    then(0, to_opp)
    prepare(2)

    def near_field(c, first, signals):
        wide = jnp.concatenate(signals, axis=1)
        weights = jnp.concatenate([near[c, first + i] for i in range(len(signals))], axis=1)
        return nt(wide, weights)

    for c in range(CL):
        low, high = max(c - 1, 0), min(c + 1, CL - 1)
        total[c] = near_field(c, low - c + 1, [sig[i] for i in range(low, high + 1)])

    now(early_opp, halo_opp)
    now(early_edge, halo_edge)
    to_opp.wait_recv()
    b1 = spread_first(own, other_start)
    pl.when(early_opp)(halo_opp.start)
    then(1, halo_edge)

    low, high = pl.ds(other_start, 2), pl.ds(other_start + 2, 2)

    def forward(at):
        return send_all([(own.at[at], neighbour.at[at], near_z)])

    b2 = spread_second(own, other_start, b1)
    fwd = forward((x, slice(None), low)) + forward((slice(None), y, high))
    arrived(a2)
    s_all = send_all([(own.at[:, :, mine], sibling.at[:, :, mine], sib)])
    for i in range(max(nx, ny) - 1):
        if i < nx - 1:
            b2[i].wait_recv()
            fwd += forward(((x + nx - ring(nx)[i]) % nx, slice(None), low))
        if i < ny - 1:
            b2[nx - 1 + i].wait_recv()
            fwd += forward((slice(None), (y + ny - ring(ny)[i]) % ny, high))
    other = pl.ds(other_start, CL)
    s_all += send_all([(own.at[:, :, other], sibling.at[:, :, other], sib)])
    multiply(0, own)
    arrived(s_all)
    multiply(1, sibling)
    arrived(n2)
    arrived(fwd)
    multiply(2, neighbour)

    halo_opp.wait_recv()
    halo_edge.wait_recv()
    left = jnp.where(linear == 0, jnp.zeros_like(zero), halo[0])
    right = jnp.where(linear == count - 1, jnp.zeros_like(zero), halo[1])
    total[0] += near_field(0, 0, [left])
    total[CL - 1] += near_field(CL - 1, 2, [right])

    both = acc[0 : CL * R] + pltpu.roll(acc[CL * R :], R, 1)
    far = both[:, 0:R].astype(BF16)
    for c in range(CL):
        part = lax.dot_general(
            far[c * R : (c + 1) * R], leaf_perm[c], (((0,), (0,)), ((), ())),
            preferred_element_type=F32,
        )
        out_ref[c] = (total[c] + part).astype(BF16)
    for copy in everything:
        copy.wait_send()


def per_device(nx, ny, nz, signal, leaf_basis, near_blocks, coupling, block_cols, block_rows, block_live):
    index = pltpu.SMEM((3 * GSLOTS,), jnp.int32)
    hbm = pl.BlockSpec(memory_space=pltpu.HBM)
    panel = pltpu.VMEM((nx, ny, 2 * CL, HALF, LANES), BF16)
    copies = 64
    return pl.pallas_call(
        functools.partial(kernel, nx, ny, nz),
        name="h2_product",
        out_shape=jax.ShapeDtypeStruct((CL, R, LEAF), BF16),
        in_specs=[hbm] * 7,
        out_specs=pl.BlockSpec(memory_space=pltpu.VMEM),
        scratch_shapes=[
            index, index, index,
            pltpu.VMEM((CL, R, LEAF), BF16),
            pltpu.VMEM((CL, R, LEAF), BF16),
            pltpu.VMEM((CL, 3, LEAF, LEAF), BF16),
            pltpu.VMEM((3 * GSLOTS, R * R), BF16),
            panel, panel, panel,
            pltpu.VMEM((2, R, LEAF), BF16),
            pltpu.VMEM((3, 2 * CL * R, GSLOTS * HALF), BF16),
            pltpu.VMEM((GSLOTS * HALF, LANES), BF16),
            pltpu.VMEM((2 * CL * R, LANES), F32),
            pltpu.VMEM((CL, R, LEAF), F32),
            pltpu.VMEM((512, 512), BF16),
            pltpu.VMEM((512, 512), BF16),
            pltpu.VMEM((CL, R, LEAF), BF16),
            pltpu.SemaphoreType.DMA((7,)),
            pltpu.SemaphoreType.DMA((copies,)),
            pltpu.SemaphoreType.DMA((copies,)),
            pltpu.SemaphoreType.REGULAR((3,)),
        ],
        compiler_params=pltpu.CompilerParams(
            collective_id=0, has_side_effects=True, vmem_limit_bytes=60 * 2**20
        ),
    )(block_cols, block_rows, block_live, signal, leaf_basis, near_blocks, coupling)


def solution(mesh, nx=SIDE, ny=SIDE):
    both = ("grp", "row")
    in_specs = (
        P(both, None, None), P(both, None, None), P(both, None, None, None), P(both, None),
        P(both), P(both), P(both),
    )
    nz = mesh.shape["grp"] // 2
    return jax.shard_map(
        functools.partial(per_device, nx, ny, nz), mesh=mesh, in_specs=in_specs,
        out_specs=P(both, None, None), check_vma=False,
    )
```

```python
import functools

import jax
import jax.numpy as jnp
from jax import lax
from jax.experimental import pallas as pl
from jax.experimental.pallas import tpu as pltpu
from jax.sharding import PartitionSpec as P

MESH = pl.DeviceIdType.MESH
F32 = jnp.float32
BF16 = jnp.bfloat16

CL = 4
R = 64
LEAF = 128
GSLOTS = 64
HALF = 32
LANES = 128
SIDE = 4


def one_hot(rows, columns, chosen):
    row = lax.broadcasted_iota(jnp.int32, (rows, columns), 0)
    column = lax.broadcasted_iota(jnp.int32, (rows, columns), 1)
    return jnp.where(column == chosen(row), 1.0, 0.0).astype(BF16)


def ring(n):
    return sorted(range(1, n), key=lambda d: min(d, n - d))


def nt(a, b):
    return lax.dot_general(a, b, (((1,), (1,)), ((), ())), preferred_element_type=F32)


def nn(a, b):
    return jnp.dot(a, b, preferred_element_type=F32)


def kernel(
    nx, ny, nz,
    cols_hbm, rows_hbm, live_hbm, sig_hbm, leaf_hbm, near_hbm, coup_hbm, out_ref,
    cols_ref, rows_ref, live_ref,
    sig, leaf, near, coup, own, sibling, neighbour, halo,
    lhs, gathered, acc, total, perm1, perm2, leaf_perm,
    local_sem, send_sem, recv_sem, hello,
):
    grp = lax.axis_index("grp")
    row = lax.axis_index("row")
    n_grp, n_row = 2 * nz, 2 * nx * ny
    z, core = grp // 2, grp % 2
    xy, plane = row // 2, row % 2
    x, y = xy // ny, xy % ny

    def device(x_, y_, plane_):
        return (grp, (x_ * ny + y_) * 2 + plane_)

    opposite = device(x, y, 1 - plane)
    sib = (z * 2 + 1 - core, row)
    step = 2 * core - 1
    z_here = plane * nz + z
    z_next = (z_here + step + 2 * nz) % (2 * nz)
    next_plane = z_next // nz
    next_grp = (z_next % nz) * 2 + 1 - core
    near_z = (next_grp, xy * 2 + next_plane)
    x_peers = [((x + d) % nx, device((x + d) % nx, y, plane)) for d in ring(nx)]
    y_peers = [((y + d) % ny, device(x, (y + d) % ny, plane)) for d in ring(ny)]
    linear = grp * n_row + row
    count = n_grp * n_row
    after, before = (linear + 1) % count, (linear + count - 1) % count
    edge = jnp.where(plane == 0, before, after)
    edge_dev = (edge // n_row, edge % n_row)

    def key(z_, plane_):
        return jnp.where(plane_ == 0, z_, nz)

    here = key(z, plane)
    k_opp, k_edge = key(z, 1 - plane), key(edge_dev[0] // 2, 1 - plane)
    k_near = key(z_next % nz, next_plane)
    pairs = [
        (opposite, here < k_opp, here > k_opp),
        (edge_dev, here < k_edge, here > k_edge),
        (near_z, here + 1 < k_near, here > k_near + 1),
    ]
    early_opp, early_edge, early_near = [early for _, early, _ in pairs]
    late_near = pairs[2][2]
    special = early_near
    giver = jnp.logical_and(plane == 0, linear // n_row == n_grp - 1)
    taker = (jnp.where(giver, 0, grp), jnp.where(giver, row, opposite[1]))

    mine = pl.ds(plane * CL, CL)
    other_start = (1 - plane) * CL

    stage = []
    loads = ((leaf_hbm, leaf), (sig_hbm, sig), (coup_hbm, coup), (near_hbm, near),
             (cols_hbm, cols_ref), (rows_hbm, rows_ref), (live_hbm, live_ref))
    for i, (src, dst) in enumerate(loads):
        stage.append(pltpu.make_async_copy(src, dst, local_sem.at[i]))
        stage[-1].start()

    barrier = pltpu.get_barrier_semaphore()

    def greet(semaphore, dev):
        pl.semaphore_signal(semaphore, inc=1, device_id=dev, device_id_type=MESH)

    friends = [sib] + [dev for _, dev in x_peers] + [dev for _, dev in y_peers]
    expected = len(friends)
    for friend in friends:
        greet(barrier, friend)
    for dev, early, late in pairs:
        pl.when(jnp.logical_not(late))(functools.partial(greet, barrier, dev))
        expected = expected + jnp.where(early, 0, 1)
    pl.when(special)(functools.partial(greet, barrier, (n_grp - 1, row)))
    expected = expected + jnp.where(giver, 1, 0)

    pl.semaphore_wait(barrier, expected)
    for i, (dev, _, late) in enumerate(pairs):
        pl.when(late)(functools.partial(greet, hello.at[i], dev))

    stage[0].wait()
    stage[1].wait()
    zero = jnp.zeros((R, LEAF), BF16)
    for c in range(CL):
        a = jnp.concatenate([leaf[c, 0:HALF], leaf[c, HALF : 2 * HALF]], axis=1)
        s = sig[c]
        b = jnp.concatenate(
            [jnp.concatenate([s, zero], axis=1), jnp.concatenate([zero, s], axis=1)], axis=0
        )
        own[x, y, plane * CL + c] = nt(a, b).astype(BF16)

    slots = [0]
    everything = []

    def prepared(src, dst, dev, when=None):
        i = slots[0]
        slots[0] += 1
        copy = pltpu.make_async_remote_copy(
            src_ref=src, dst_ref=dst, send_sem=send_sem.at[i], recv_sem=recv_sem.at[i],
            device_id=dev, device_id_type=MESH,
        )
        everything.append((copy, when))
        return copy

    def send_all(items):
        copies = [prepared(*item) for item in items]
        for copy in copies:
            copy.start()
        return copies

    def arrived(copies):
        for copy in copies:
            copy.wait_recv()

    block = own.at[x, y, mine]
    n_dst = neighbour.at[x, y, mine]
    to_opp = prepared(block, block, opposite)
    to_near = prepared(block, n_dst, near_z)
    opp_slot = plane
    halo_opp = prepared(sig.at[(1 - plane) * (CL - 1)], halo.at[opp_slot], opposite)
    halo_edge = prepared(sig.at[plane * (CL - 1)], halo.at[1 - opp_slot], edge_dev)

    def now(early, *copies):
        @pl.when(jnp.logical_not(early))
        def _():
            for copy in copies:
                copy.start()

    def then(i, *copies):
        @pl.when(pairs[i][1])
        def _():
            pl.semaphore_wait(hello.at[i], 1)
            for copy in copies:
                copy.start()

    def first_copies(panel, start, when=None):
        low, high = pl.ds(start, 2), pl.ds(start + 2, 2)
        return (
            [prepared(panel.at[x, y, low], panel.at[x, y, low], dev, when) for _, dev in y_peers],
            [prepared(panel.at[x, y, high], panel.at[x, y, high], dev, when) for _, dev in x_peers],
        )

    def second_copies(panel, start, when=None):
        low, high = panel.at[x, :, pl.ds(start, 2)], panel.at[:, y, pl.ds(start + 2, 2)]
        return (
            [prepared(low, low, dev, when) for _, dev in x_peers],
            [prepared(high, high, dev, when) for _, dev in y_peers],
        )

    def begin(copies):
        for copy in copies:
            copy.start()

    def pass_on(first, second):
        for got, give in zip(first, second):
            arrived(got)
            begin(give)

    to_taker = prepared(block, n_dst, taker, giver)
    now(early_opp, to_opp)
    pl.when(giver)(to_taker.start)
    now(early_near, to_near)
    my_start, next_start = plane * CL, next_plane * CL
    a1, a2 = first_copies(own, my_start), second_copies(own, my_start)
    n1, n2 = first_copies(neighbour, next_start), second_copies(neighbour, next_start)
    b1 = first_copies(own, other_start)
    next_other = (1 - next_plane) * CL
    t1, t2 = first_copies(neighbour, next_other, special), second_copies(neighbour, next_other, special)
    begin(a1[0] + a1[1])

    t_count, a_count, j_count = 16, 4, 32
    size = t_count * j_count
    perm1[...] = one_hot(size, size, lambda r: (r % j_count) * t_count + r // j_count)

    def column_of(c):
        kp, h, rest = c // 256, (c // 128) % 2, c % 128
        return (rest // HALF) * 128 + kp * 64 + h * HALF + rest % HALF

    r_i = lax.broadcasted_iota(jnp.int32, (size, size), 0)
    c_i = lax.broadcasted_iota(jnp.int32, (size, size), 1)
    perm2[...] = jnp.where(r_i == column_of(c_i), 1.0, 0.0).astype(BF16)
    reorder = one_hot(R, R, lambda r: (r % HALF) * 2 + r // HALF)
    for c in range(CL):
        leaf_perm[c] = nn(reorder, leaf[c]).astype(BF16)

    places = (1, jnp.where(core == 0, 2, 0), jnp.where(core == 0, 0, 2))

    def prepare(s):
        first = pl.multiple_of(places[s] * GSLOTS, GSLOTS)
        x_rows = []
        for j in range(j_count):
            x_rows.append(jnp.concatenate(
                [coup[pl.ds(first + a * t_count, t_count), j * LANES : (j + 1) * LANES]
                 for a in range(a_count)], axis=1))
        xs = jnp.concatenate(x_rows, axis=0)
        ys = nn(perm1[...], xs).astype(BF16)
        ws = nn(ys, perm2[...]).astype(BF16)
        lane_slot = lax.broadcasted_iota(jnp.int32, (1, LANES), 1) // HALF
        for t in range(t_count):
            code = jnp.full((1, LANES), -1, jnp.int32)
            for a in range(a_count):
                b = first + a * t_count + t
                slot_row = jnp.where(live_ref[b] != 0, rows_ref[b], -1)
                code = jnp.where(lane_slot == a, slot_row, code)
            for i in range(CL):
                mask = jnp.where(code == i, 1.0, 0.0)
                mask = jnp.broadcast_to(mask, (j_count, LANES)).astype(BF16)
                for kp in range(2):
                    for h in range(2):
                        tile = ws[t * j_count : (t + 1) * j_count,
                                  (kp * 2 + h) * LANES : (kp * 2 + h + 1) * LANES]
                        lhs[s, (h * CL + i) * R + kp * HALF : (h * CL + i) * R + (kp + 1) * HALF,
                            t * LANES : (t + 1) * LANES] = tile * mask

    def multiply(s, panel):
        first = places[s] * GSLOTS
        for t in range(t_count):
            for a in range(a_count):
                c = lax.rem(cols_ref[first + a * t_count + t], n_row * CL)
                at = (t * a_count + a) * HALF
                gathered[at : at + HALF] = panel[c // (8 * ny), (c // 8) % ny, c % 8]
        part = nn(lhs[s], gathered[...])
        if s == 0:
            acc[...] = part
        else:
            acc[...] += part

    for copy in stage[2:]:
        copy.wait()
    prepare(0)
    pass_on(a1, a2)

    then(2, to_near)
    to_near.wait_recv()
    begin(n1[0] + n1[1])
    prepare(1)
    then(0, to_opp)

    def far_step():
        to_opp.wait_recv()
        begin(b1[0] + b1[1])

    @pl.when(special)
    def _():
        to_taker.wait_recv()
        begin(t1[0] + t1[1])
        far_step()

    pass_on(n1, n2)
    prepare(2)
    halo_opp.start()
    then(1, halo_edge)
    now(early_edge, halo_edge)

    def near_field(c, first, signals):
        wide = jnp.concatenate(signals, axis=1)
        weights = jnp.concatenate([near[c, first + i] for i in range(len(signals))], axis=1)
        return nt(wide, weights)

    for c in range(CL):
        low, high = max(c - 1, 0), min(c + 1, CL - 1)
        total[c] = near_field(c, low - c + 1, [sig[i] for i in range(low, high + 1)])

    pl.when(jnp.logical_not(special))(far_step)

    start = other_start
    usual = jnp.logical_not(special)
    forwards = jnp.logical_not(late_near)
    pair_low, pair_high = pl.ds(start, 2), pl.ds(start + 2, 2)
    every = slice(None)

    def forward(at):
        copy = prepared(own.at[at], neighbour.at[at], near_z, forwards)
        pl.when(forwards)(copy.start)
        return [copy]

    def share(at):
        return send_all([(own.at[at], sibling.at[at], sib)])

    arrived(b1[0])
    line = own.at[x, :, pair_low]
    b2x = send_all([(line, line, dev) for _, dev in x_peers])
    f_low, = forward((x, every, pair_low))
    arrived(b1[1])
    line = own.at[:, y, pair_high]
    b2y = send_all([(line, line, dev) for _, dev in y_peers])
    f_high, = forward((every, y, pair_high))
    s_all = share((x, every, pair_low)) + share((every, y, pair_high))
    arrived(a2[0] + a2[1])
    s_all += share((every, every, mine))
    m_low = neighbour.at[x, :, pl.ds(next_other, 1)]
    m_high = neighbour.at[:, y, pl.ds(next_other + 2, 1)]
    m2 = (
        [prepared(m_low, m_low, dev, usual) for _, dev in x_peers],
        [prepared(m_high, m_high, dev, usual) for _, dev in y_peers],
    )

    def spread_next():
        pass_on(([f_low], [f_high]), m2)

    pl.when(usual)(spread_next)
    pl.when(special)(functools.partial(pass_on, t1, t2))
    fwd = []
    for i in range(max(nx, ny) - 1):
        if i < nx - 1:
            b2x[i].wait_recv()
            px = (x + nx - ring(nx)[i]) % nx
            fwd += forward((px, every, pl.ds(start + 1, 1)))
            s_all += share((px, every, pair_low))
        if i < ny - 1:
            b2y[i].wait_recv()
            py = (y + ny - ring(ny)[i]) % ny
            fwd += forward((every, py, pl.ds(start + 3, 1)))
            s_all += share((every, py, pair_high))
    multiply(0, own)
    arrived(s_all)
    multiply(1, sibling)
    arrived(n2[0] + n2[1])
    pl.when(usual)(functools.partial(arrived, m2[0] + m2[1] + fwd))
    pl.when(special)(functools.partial(arrived, t2[0] + t2[1]))
    multiply(2, neighbour)

    halo_opp.wait_recv()
    halo_edge.wait_recv()
    left = jnp.where(linear == 0, jnp.zeros_like(zero), halo[0])
    right = jnp.where(linear == count - 1, jnp.zeros_like(zero), halo[1])
    total[0] += near_field(0, 0, [left])
    total[CL - 1] += near_field(CL - 1, 2, [right])

    both = acc[0 : CL * R] + pltpu.roll(acc[CL * R :], R, 1)
    far = both[:, 0:R].astype(BF16)
    for c in range(CL):
        part = lax.dot_general(
            far[c * R : (c + 1) * R], leaf_perm[c], (((0,), (0,)), ((), ())),
            preferred_element_type=F32,
        )
        out_ref[c] = (total[c] + part).astype(BF16)
    for copy, when in everything:
        if when is None:
            copy.wait_send()
        else:
            pl.when(when)(copy.wait_send)


def per_device(nx, ny, nz, signal, leaf_basis, near_blocks, coupling, block_cols, block_rows, block_live):
    index = pltpu.SMEM((3 * GSLOTS,), jnp.int32)
    hbm = pl.BlockSpec(memory_space=pltpu.HBM)
    panel = pltpu.VMEM((nx, ny, 2 * CL, HALF, LANES), BF16)
    copies = 96
    return pl.pallas_call(
        functools.partial(kernel, nx, ny, nz),
        name="h2_product",
        out_shape=jax.ShapeDtypeStruct((CL, R, LEAF), BF16),
        in_specs=[hbm] * 7,
        out_specs=pl.BlockSpec(memory_space=pltpu.VMEM),
        scratch_shapes=[
            index, index, index,
            pltpu.VMEM((CL, R, LEAF), BF16),
            pltpu.VMEM((CL, R, LEAF), BF16),
            pltpu.VMEM((CL, 3, LEAF, LEAF), BF16),
            pltpu.VMEM((3 * GSLOTS, R * R), BF16),
            panel, panel, panel,
            pltpu.VMEM((2, R, LEAF), BF16),
            pltpu.VMEM((3, 2 * CL * R, GSLOTS * HALF), BF16),
            pltpu.VMEM((GSLOTS * HALF, LANES), BF16),
            pltpu.VMEM((2 * CL * R, LANES), F32),
            pltpu.VMEM((CL, R, LEAF), F32),
            pltpu.VMEM((512, 512), BF16),
            pltpu.VMEM((512, 512), BF16),
            pltpu.VMEM((CL, R, LEAF), BF16),
            pltpu.SemaphoreType.DMA((7,)),
            pltpu.SemaphoreType.DMA((copies,)),
            pltpu.SemaphoreType.DMA((copies,)),
            pltpu.SemaphoreType.REGULAR((3,)),
        ],
        compiler_params=pltpu.CompilerParams(
            collective_id=0, has_side_effects=True, vmem_limit_bytes=60 * 2**20
        ),
    )(block_cols, block_rows, block_live, signal, leaf_basis, near_blocks, coupling)


def solution(mesh, nx=SIDE, ny=SIDE):
    both = ("grp", "row")
    in_specs = (
        P(both, None, None), P(both, None, None), P(both, None, None, None), P(both, None),
        P(both), P(both), P(both),
    )
    nz = mesh.shape["grp"] // 2
    return jax.shard_map(
        functools.partial(per_device, nx, ny, nz), mesh=mesh, in_specs=in_specs,
        out_specs=P(both, None, None), check_vma=False,
    )
```

```python
import functools

import jax
import jax.numpy as jnp
from jax import lax
from jax.experimental import pallas as pl
from jax.experimental.pallas import tpu as pltpu
from jax.sharding import PartitionSpec as P

MESH = pl.DeviceIdType.MESH
F32 = jnp.float32
BF16 = jnp.bfloat16

CL = 4
R = 64
LEAF = 128
GSLOTS = 64
HALF = 32
LANES = 128
SIDE = 4


def one_hot(rows, columns, chosen):
    row = lax.broadcasted_iota(jnp.int32, (rows, columns), 0)
    column = lax.broadcasted_iota(jnp.int32, (rows, columns), 1)
    return jnp.where(column == chosen(row), 1.0, 0.0).astype(BF16)


def ring(n):
    return sorted(range(1, n), key=lambda d: min(d, n - d))


def nt(a, b):
    return lax.dot_general(a, b, (((1,), (1,)), ((), ())), preferred_element_type=F32)


def nn(a, b):
    return jnp.dot(a, b, preferred_element_type=F32)


def kernel(
    nx, ny, nz,
    cols_hbm, rows_hbm, live_hbm, sig_hbm, leaf_hbm, near_hbm, coup_hbm, out_ref,
    cols_ref, rows_ref, live_ref,
    sig, leaf, near, coup, own, sibling, neighbour, halo,
    lhs, gathered, acc, total, perm1, perm2, leaf_perm,
    local_sem, send_sem, recv_sem, hello,
):
    grp = lax.axis_index("grp")
    row = lax.axis_index("row")
    n_grp, n_row = 2 * nz, 2 * nx * ny
    z, core = grp // 2, grp % 2
    xy, plane = row // 2, row % 2
    x, y = xy // ny, xy % ny

    def device(x_, y_, plane_):
        return (grp, (x_ * ny + y_) * 2 + plane_)

    opposite = device(x, y, 1 - plane)
    sib = (z * 2 + 1 - core, row)
    step = 2 * core - 1
    z_here = plane * nz + z
    z_next = (z_here + step + 2 * nz) % (2 * nz)
    next_plane = z_next // nz
    next_grp = (z_next % nz) * 2 + 1 - core
    near_z = (next_grp, xy * 2 + next_plane)
    x_peers = [((x + d) % nx, device((x + d) % nx, y, plane)) for d in ring(nx)]
    y_peers = [((y + d) % ny, device(x, (y + d) % ny, plane)) for d in ring(ny)]
    linear = grp * n_row + row
    count = n_grp * n_row
    after, before = (linear + 1) % count, (linear + count - 1) % count
    edge = jnp.where(plane == 0, before, after)
    edge_dev = (edge // n_row, edge % n_row)

    def key(z_, plane_):
        return jnp.where(plane_ == 0, z_, nz)

    here = key(z, plane)
    k_opp, k_edge = key(z, 1 - plane), key(edge_dev[0] // 2, 1 - plane)
    k_near = key(z_next % nz, next_plane)
    pairs = [
        (opposite, here < k_opp, here > k_opp),
        (edge_dev, here < k_edge, here > k_edge),
        (near_z, here + 1 < k_near, here > k_near + 1),
    ]
    early_opp, early_edge, early_near = [early for _, early, _ in pairs]
    late_near = pairs[2][2]
    special = early_near
    giver = jnp.logical_and(plane == 0, linear // n_row == n_grp - 1)
    taker = (jnp.where(giver, 0, grp), jnp.where(giver, row, opposite[1]))

    mine = pl.ds(plane * CL, CL)
    other_start = (1 - plane) * CL

    stage = []
    loads = ((leaf_hbm, leaf), (sig_hbm, sig), (coup_hbm, coup), (near_hbm, near),
             (cols_hbm, cols_ref), (rows_hbm, rows_ref), (live_hbm, live_ref))
    for i, (src, dst) in enumerate(loads):
        stage.append(pltpu.make_async_copy(src, dst, local_sem.at[i]))
        stage[-1].start()

    barrier = pltpu.get_barrier_semaphore()

    def greet(semaphore, dev):
        pl.semaphore_signal(semaphore, inc=1, device_id=dev, device_id_type=MESH)

    friends = [sib] + [dev for _, dev in x_peers] + [dev for _, dev in y_peers]
    expected = len(friends)
    for friend in friends:
        greet(barrier, friend)
    for dev, early, late in pairs:
        pl.when(jnp.logical_not(late))(functools.partial(greet, barrier, dev))
        expected = expected + jnp.where(early, 0, 1)
    pl.when(special)(functools.partial(greet, barrier, (n_grp - 1, row)))
    expected = expected + jnp.where(giver, 1, 0)

    pl.semaphore_wait(barrier, expected)
    for i, (dev, _, late) in enumerate(pairs):
        pl.when(late)(functools.partial(greet, hello.at[i], dev))

    stage[0].wait()
    stage[1].wait()
    zero = jnp.zeros((R, LEAF), BF16)
    for c in range(CL):
        a = jnp.concatenate([leaf[c, 0:HALF], leaf[c, HALF : 2 * HALF]], axis=1)
        s = sig[c]
        b = jnp.concatenate(
            [jnp.concatenate([s, zero], axis=1), jnp.concatenate([zero, s], axis=1)], axis=0
        )
        own[x, y, plane * CL + c] = nt(a, b).astype(BF16)

    slots = [0]
    everything = []

    def prepared(src, dst, dev, when=None):
        i = slots[0]
        slots[0] += 1
        copy = pltpu.make_async_remote_copy(
            src_ref=src, dst_ref=dst, send_sem=send_sem.at[i], recv_sem=recv_sem.at[i],
            device_id=dev, device_id_type=MESH,
        )
        everything.append((copy, when))
        return copy

    def send_all(items):
        copies = [prepared(*item) for item in items]
        for copy in copies:
            copy.start()
        return copies

    def arrived(copies):
        for copy in copies:
            copy.wait_recv()

    block = own.at[x, y, mine]
    n_dst = neighbour.at[x, y, mine]
    to_opp = prepared(block, block, opposite)
    to_near = prepared(block, n_dst, near_z)
    opp_slot = plane
    halo_opp = prepared(sig.at[(1 - plane) * (CL - 1)], halo.at[opp_slot], opposite)
    halo_edge = prepared(sig.at[plane * (CL - 1)], halo.at[1 - opp_slot], edge_dev)

    def now(early, *copies):
        @pl.when(jnp.logical_not(early))
        def _():
            for copy in copies:
                copy.start()

    def then(i, *copies):
        @pl.when(pairs[i][1])
        def _():
            pl.semaphore_wait(hello.at[i], 1)
            for copy in copies:
                copy.start()

    def first_copies(panel, start, when=None):
        low, high = pl.ds(start, 2), pl.ds(start + 2, 2)
        return (
            [prepared(panel.at[x, y, low], panel.at[x, y, low], dev, when) for _, dev in y_peers],
            [prepared(panel.at[x, y, high], panel.at[x, y, high], dev, when) for _, dev in x_peers],
        )

    def second_copies(panel, start, when=None):
        low, high = panel.at[x, :, pl.ds(start, 2)], panel.at[:, y, pl.ds(start + 2, 2)]
        return (
            [prepared(low, low, dev, when) for _, dev in x_peers],
            [prepared(high, high, dev, when) for _, dev in y_peers],
        )

    def begin(copies):
        for copy in copies:
            copy.start()

    def pass_on(first, second):
        for got, give in zip(first, second):
            arrived(got)
            begin(give)

    to_taker = prepared(block, n_dst, taker, giver)
    now(early_opp, to_opp)
    pl.when(giver)(to_taker.start)
    now(early_near, to_near)
    my_start, next_start = plane * CL, next_plane * CL
    a1, a2 = first_copies(own, my_start), second_copies(own, my_start)
    n1, n2 = first_copies(neighbour, next_start), second_copies(neighbour, next_start)
    b1 = first_copies(own, other_start)
    next_other = (1 - next_plane) * CL
    t1, t2 = first_copies(neighbour, next_other, special), second_copies(neighbour, next_other, special)
    begin(a1[0] + a1[1])

    t_count, a_count, j_count = 16, 4, 32
    size = t_count * j_count
    perm1[...] = one_hot(size, size, lambda r: (r % j_count) * t_count + r // j_count)

    def column_of(c):
        kp, h, rest = c // 256, (c // 128) % 2, c % 128
        return (rest // HALF) * 128 + kp * 64 + h * HALF + rest % HALF

    r_i = lax.broadcasted_iota(jnp.int32, (size, size), 0)
    c_i = lax.broadcasted_iota(jnp.int32, (size, size), 1)
    perm2[...] = jnp.where(r_i == column_of(c_i), 1.0, 0.0).astype(BF16)
    reorder = one_hot(R, R, lambda r: (r % HALF) * 2 + r // HALF)
    for c in range(CL):
        leaf_perm[c] = nn(reorder, leaf[c]).astype(BF16)

    places = (1, jnp.where(core == 0, 2, 0), jnp.where(core == 0, 0, 2))

    def prepare(s):
        first = pl.multiple_of(places[s] * GSLOTS, GSLOTS)
        x_rows = []
        for j in range(j_count):
            x_rows.append(jnp.concatenate(
                [coup[pl.ds(first + a * t_count, t_count), j * LANES : (j + 1) * LANES]
                 for a in range(a_count)], axis=1))
        xs = jnp.concatenate(x_rows, axis=0)
        ys = nn(perm1[...], xs).astype(BF16)
        ws = nn(ys, perm2[...]).astype(BF16)
        lane_slot = lax.broadcasted_iota(jnp.int32, (1, LANES), 1) // HALF
        for t in range(t_count):
            code = jnp.full((1, LANES), -1, jnp.int32)
            for a in range(a_count):
                b = first + a * t_count + t
                slot_row = jnp.where(live_ref[b] != 0, rows_ref[b], -1)
                code = jnp.where(lane_slot == a, slot_row, code)
            for i in range(CL):
                mask = jnp.where(code == i, 1.0, 0.0)
                mask = jnp.broadcast_to(mask, (j_count, LANES)).astype(BF16)
                for kp in range(2):
                    for h in range(2):
                        tile = ws[t * j_count : (t + 1) * j_count,
                                  (kp * 2 + h) * LANES : (kp * 2 + h + 1) * LANES]
                        lhs[s, (h * CL + i) * R + kp * HALF : (h * CL + i) * R + (kp + 1) * HALF,
                            t * LANES : (t + 1) * LANES] = tile * mask

    def multiply(s, panel):
        first = places[s] * GSLOTS
        x_shift = 3 + ny.bit_length() - 1
        for t in range(t_count):
            for a in range(a_count):
                c = cols_ref[first + a * t_count + t]
                at = (t * a_count + a) * HALF
                gathered[at : at + HALF] = panel[
                    (c >> x_shift) & (nx - 1), (c >> 3) & (ny - 1), c & (2 * CL - 1)
                ]
        part = nn(lhs[s], gathered[...])
        if s == 0:
            acc[...] = part
        else:
            acc[...] += part

    for copy in stage[2:]:
        copy.wait()
    prepare(0)
    pass_on(a1, a2)


    def pair_up():
        then(0, to_opp)

    pl.when(special)(pair_up)
    then(2, to_near)
    to_near.wait_recv()
    begin(n1[0] + n1[1])
    prepare(1)
    pl.when(jnp.logical_not(special))(pair_up)

    def far_step():
        to_opp.wait_recv()
        begin(b1[0] + b1[1])

    @pl.when(special)
    def _():
        to_taker.wait_recv()
        begin(t1[0] + t1[1])
        far_step()

    pass_on(n1, n2)
    prepare(2)
    now(early_opp, halo_opp)
    now(early_edge, halo_edge)

    def near_field(c, first, signals):
        wide = jnp.concatenate(signals, axis=1)
        weights = jnp.concatenate([near[c, first + i] for i in range(len(signals))], axis=1)
        return nt(wide, weights)

    for c in range(CL):
        low, high = max(c - 1, 0), min(c + 1, CL - 1)
        total[c] = near_field(c, low - c + 1, [sig[i] for i in range(low, high + 1)])

    pl.when(jnp.logical_not(special))(far_step)

    start = other_start
    usual = jnp.logical_not(special)
    forwards = jnp.logical_not(late_near)
    pair_low, pair_high = pl.ds(start, 2), pl.ds(start + 2, 2)
    every = slice(None)

    def forward(at):
        copy = prepared(own.at[at], neighbour.at[at], near_z, forwards)
        pl.when(forwards)(copy.start)
        return [copy]

    def share(at):
        return send_all([(own.at[at], sibling.at[at], sib)])

    arrived(b1[0])
    line = own.at[x, :, pair_low]
    b2x = send_all([(line, line, dev) for _, dev in x_peers])
    f_low, = forward((x, every, pair_low))
    arrived(b1[1])
    line = own.at[:, y, pair_high]
    b2y = send_all([(line, line, dev) for _, dev in y_peers])
    f_high, = forward((every, y, pair_high))
    pl.when(early_opp)(halo_opp.start)
    then(1, halo_edge)
    s_all = share((x, every, pair_low)) + share((every, y, pair_high))
    arrived(a2[0] + a2[1])
    s_all += share((every, every, mine))
    m_low = neighbour.at[x, :, pl.ds(next_other, 1)]
    m_high = neighbour.at[:, y, pl.ds(next_other + 2, 1)]
    m2 = (
        [prepared(m_low, m_low, dev, usual) for _, dev in x_peers],
        [prepared(m_high, m_high, dev, usual) for _, dev in y_peers],
    )

    def spread_next():
        pass_on(([f_low], [f_high]), m2)

    pl.when(usual)(spread_next)
    pl.when(special)(functools.partial(pass_on, t1, t2))
    fwd = []
    for i in range(max(nx, ny) - 1):
        if i < nx - 1:
            b2x[i].wait_recv()
            px = (x + nx - ring(nx)[i]) % nx
            fwd += forward((px, every, pl.ds(start + 1, 1)))
            s_all += share((px, every, pair_low))
        if i < ny - 1:
            b2y[i].wait_recv()
            py = (y + ny - ring(ny)[i]) % ny
            fwd += forward((every, py, pl.ds(start + 3, 1)))
            s_all += share((every, py, pair_high))
    def multiply_next():
        arrived(n2[0] + n2[1])
        pl.when(usual)(functools.partial(arrived, m2[0] + m2[1] + fwd))
        pl.when(special)(functools.partial(arrived, t2[0] + t2[1]))
        multiply(2, neighbour)

    multiply(0, own)
    first_plane = jnp.logical_and(plane == 0, z == 0)
    pl.when(first_plane)(multiply_next)
    arrived(s_all)
    multiply(1, sibling)
    pl.when(jnp.logical_not(first_plane))(multiply_next)

    halo_opp.wait_recv()
    halo_edge.wait_recv()
    left = jnp.where(linear == 0, jnp.zeros_like(zero), halo[0])
    right = jnp.where(linear == count - 1, jnp.zeros_like(zero), halo[1])
    total[0] += near_field(0, 0, [left])
    total[CL - 1] += near_field(CL - 1, 2, [right])

    both = acc[0 : CL * R] + pltpu.roll(acc[CL * R :], R, 1)
    far = both[:, 0:R].astype(BF16)
    for c in range(CL):
        part = lax.dot_general(
            far[c * R : (c + 1) * R], leaf_perm[c], (((0,), (0,)), ((), ())),
            preferred_element_type=F32,
        )
        out_ref[c] = (total[c] + part).astype(BF16)
    for copy, when in everything:
        if when is None:
            copy.wait_send()
        else:
            pl.when(when)(copy.wait_send)


def per_device(nx, ny, nz, signal, leaf_basis, near_blocks, coupling, block_cols, block_rows, block_live):
    index = pltpu.SMEM((3 * GSLOTS,), jnp.int32)
    hbm = pl.BlockSpec(memory_space=pltpu.HBM)
    panel = pltpu.VMEM((nx, ny, 2 * CL, HALF, LANES), BF16)
    copies = 96
    return pl.pallas_call(
        functools.partial(kernel, nx, ny, nz),
        name="h2_product",
        out_shape=jax.ShapeDtypeStruct((CL, R, LEAF), BF16),
        in_specs=[hbm] * 7,
        out_specs=pl.BlockSpec(memory_space=pltpu.VMEM),
        scratch_shapes=[
            index, index, index,
            pltpu.VMEM((CL, R, LEAF), BF16),
            pltpu.VMEM((CL, R, LEAF), BF16),
            pltpu.VMEM((CL, 3, LEAF, LEAF), BF16),
            pltpu.VMEM((3 * GSLOTS, R * R), BF16),
            panel, panel, panel,
            pltpu.VMEM((2, R, LEAF), BF16),
            pltpu.VMEM((3, 2 * CL * R, GSLOTS * HALF), BF16),
            pltpu.VMEM((GSLOTS * HALF, LANES), BF16),
            pltpu.VMEM((2 * CL * R, LANES), F32),
            pltpu.VMEM((CL, R, LEAF), F32),
            pltpu.VMEM((512, 512), BF16),
            pltpu.VMEM((512, 512), BF16),
            pltpu.VMEM((CL, R, LEAF), BF16),
            pltpu.SemaphoreType.DMA((7,)),
            pltpu.SemaphoreType.DMA((copies,)),
            pltpu.SemaphoreType.DMA((copies,)),
            pltpu.SemaphoreType.REGULAR((3,)),
        ],
        compiler_params=pltpu.CompilerParams(
            collective_id=0, has_side_effects=True, vmem_limit_bytes=60 * 2**20
        ),
    )(block_cols, block_rows, block_live, signal, leaf_basis, near_blocks, coupling)


def solution(mesh, nx=SIDE, ny=SIDE):
    both = ("grp", "row")
    in_specs = (
        P(both, None, None), P(both, None, None), P(both, None, None, None), P(both, None),
        P(both), P(both), P(both),
    )
    nz = mesh.shape["grp"] // 2
    return jax.shard_map(
        functools.partial(per_device, nx, ny, nz), mesh=mesh, in_specs=in_specs,
        out_specs=P(both, None, None), check_vma=False,
    )
```

```python
import functools

import jax
import jax.numpy as jnp
from jax import lax
from jax.experimental import pallas as pl
from jax.experimental.pallas import tpu as pltpu
from jax.sharding import PartitionSpec as P

MESH = pl.DeviceIdType.MESH
F32 = jnp.float32
BF16 = jnp.bfloat16

CL = 4
R = 64
LEAF = 128
GSLOTS = 64
HALF = 32
LANES = 128
SIDE = 4


def one_hot(rows, columns, chosen):
    row = lax.broadcasted_iota(jnp.int32, (rows, columns), 0)
    column = lax.broadcasted_iota(jnp.int32, (rows, columns), 1)
    return jnp.where(column == chosen(row), 1.0, 0.0).astype(BF16)


def ring(n):
    return sorted(range(1, n), key=lambda d: min(d, n - d))


def nt(a, b):
    return lax.dot_general(a, b, (((1,), (1,)), ((), ())), preferred_element_type=F32)


def nn(a, b):
    return jnp.dot(a, b, preferred_element_type=F32)


def kernel(
    nx, ny, nz,
    cols_hbm, rows_hbm, live_hbm, sig_hbm, leaf_hbm, near_hbm, coup_hbm, out_ref,
    cols_ref, rows_ref, live_ref,
    sig, leaf, near, coup, own, sibling, neighbour, halo,
    lhs, gathered, acc, total, perm1, perm2, leaf_perm,
    local_sem, send_sem, recv_sem, hello,
):
    grp = lax.axis_index("grp")
    row = lax.axis_index("row")
    n_grp, n_row = 2 * nz, 2 * nx * ny
    z, core = grp // 2, grp % 2
    xy, plane = row // 2, row % 2
    x, y = xy // ny, xy % ny

    def device(x_, y_, plane_):
        return (grp, (x_ * ny + y_) * 2 + plane_)

    opposite = device(x, y, 1 - plane)
    sib = (z * 2 + 1 - core, row)
    step = 2 * core - 1
    z_here = plane * nz + z
    z_next = (z_here + step + 2 * nz) % (2 * nz)
    next_plane = z_next // nz
    next_grp = (z_next % nz) * 2 + 1 - core
    near_z = (next_grp, xy * 2 + next_plane)
    x_peers = [((x + d) % nx, device((x + d) % nx, y, plane)) for d in ring(nx)]
    y_peers = [((y + d) % ny, device(x, (y + d) % ny, plane)) for d in ring(ny)]
    linear = grp * n_row + row
    count = n_grp * n_row
    after, before = (linear + 1) % count, (linear + count - 1) % count
    edge = jnp.where(plane == 0, before, after)
    edge_dev = (edge // n_row, edge % n_row)

    def key(z_, plane_):
        return jnp.where(plane_ == 0, z_, nz)

    here = key(z, plane)
    k_opp, k_edge = key(z, 1 - plane), key(edge_dev[0] // 2, 1 - plane)
    k_near = key(z_next % nz, next_plane)
    pairs = [
        (opposite, here < k_opp, here > k_opp),
        (edge_dev, here < k_edge, here > k_edge),
        (near_z, here + 1 < k_near, here > k_near + 1),
    ]
    early_opp, early_edge, early_near = [early for _, early, _ in pairs]
    late_near = pairs[2][2]
    special = early_near
    giver = jnp.logical_and(plane == 0, linear // n_row == n_grp - 1)
    taker = (jnp.where(giver, 0, grp), jnp.where(giver, row, opposite[1]))

    mine = pl.ds(plane * CL, CL)
    other_start = (1 - plane) * CL

    stage = []
    loads = ((leaf_hbm, leaf), (sig_hbm, sig), (coup_hbm, coup), (near_hbm, near),
             (cols_hbm, cols_ref), (rows_hbm, rows_ref), (live_hbm, live_ref))
    for i, (src, dst) in enumerate(loads):
        stage.append(pltpu.make_async_copy(src, dst, local_sem.at[i]))
        stage[-1].start()

    barrier = pltpu.get_barrier_semaphore()

    def greet(semaphore, dev):
        pl.semaphore_signal(semaphore, inc=1, device_id=dev, device_id_type=MESH)

    friends = [sib] + [dev for _, dev in x_peers] + [dev for _, dev in y_peers]
    expected = len(friends)
    for friend in friends:
        greet(barrier, friend)
    for dev, early, late in pairs:
        pl.when(jnp.logical_not(late))(functools.partial(greet, barrier, dev))
        expected = expected + jnp.where(early, 0, 1)
    pl.when(special)(functools.partial(greet, barrier, (n_grp - 1, row)))
    expected = expected + jnp.where(giver, 1, 0)

    pl.semaphore_wait(barrier, expected)
    for i, (dev, _, late) in enumerate(pairs):
        pl.when(late)(functools.partial(greet, hello.at[i], dev))

    stage[0].wait()
    stage[1].wait()
    zero = jnp.zeros((R, LEAF), BF16)
    for c in range(CL):
        a = jnp.concatenate([leaf[c, 0:HALF], leaf[c, HALF : 2 * HALF]], axis=1)
        s = sig[c]
        b = jnp.concatenate(
            [jnp.concatenate([s, zero], axis=1), jnp.concatenate([zero, s], axis=1)], axis=0
        )
        own[x, y, plane * CL + c] = nt(a, b).astype(BF16)

    slots = [0]
    everything = []

    def prepared(src, dst, dev, when=None):
        i = slots[0]
        slots[0] += 1
        copy = pltpu.make_async_remote_copy(
            src_ref=src, dst_ref=dst, send_sem=send_sem.at[i], recv_sem=recv_sem.at[i],
            device_id=dev, device_id_type=MESH,
        )
        everything.append((copy, when))
        return copy

    def send_all(items):
        copies = [prepared(*item) for item in items]
        for copy in copies:
            copy.start()
        return copies

    def arrived(copies):
        for copy in copies:
            copy.wait_recv()

    block = own.at[x, y, mine]
    n_dst = neighbour.at[x, y, mine]
    to_opp = prepared(block, block, opposite)
    to_near = prepared(block, n_dst, near_z)
    opp_slot = plane
    halo_opp = prepared(sig.at[(1 - plane) * (CL - 1)], halo.at[opp_slot], opposite)
    halo_edge = prepared(sig.at[plane * (CL - 1)], halo.at[1 - opp_slot], edge_dev)

    def now(early, *copies):
        @pl.when(jnp.logical_not(early))
        def _():
            for copy in copies:
                copy.start()

    def then(i, *copies):
        @pl.when(pairs[i][1])
        def _():
            pl.semaphore_wait(hello.at[i], 1)
            for copy in copies:
                copy.start()

    def first_copies(panel, start, when=None):
        low, high = pl.ds(start, 2), pl.ds(start + 2, 2)
        return (
            [prepared(panel.at[x, y, low], panel.at[x, y, low], dev, when) for _, dev in y_peers],
            [prepared(panel.at[x, y, high], panel.at[x, y, high], dev, when) for _, dev in x_peers],
        )

    def second_copies(panel, start, when=None):
        low, high = panel.at[x, :, pl.ds(start, 2)], panel.at[:, y, pl.ds(start + 2, 2)]
        return (
            [prepared(low, low, dev, when) for _, dev in x_peers],
            [prepared(high, high, dev, when) for _, dev in y_peers],
        )

    def begin(copies):
        for copy in copies:
            copy.start()

    def pass_on(first, second):
        for got, give in zip(first, second):
            arrived(got)
            begin(give)

    to_taker = prepared(block, n_dst, taker, giver)
    now(early_opp, to_opp)
    pl.when(giver)(to_taker.start)
    now(early_near, to_near)
    my_start, next_start = plane * CL, next_plane * CL
    a1, a2 = first_copies(own, my_start), second_copies(own, my_start)
    n1, n2 = first_copies(neighbour, next_start), second_copies(neighbour, next_start)
    b1 = first_copies(own, other_start)
    next_other = (1 - next_plane) * CL
    t1, t2 = first_copies(neighbour, next_other, special), second_copies(neighbour, next_other, special)
    begin(a1[0] + a1[1])

    t_count, a_count, j_count = 16, 4, 32
    size = t_count * j_count
    perm1[...] = one_hot(size, size, lambda r: (r % j_count) * t_count + r // j_count)

    def column_of(c):
        kp, h, rest = c // 256, (c // 128) % 2, c % 128
        return (rest // HALF) * 128 + kp * 64 + h * HALF + rest % HALF

    r_i = lax.broadcasted_iota(jnp.int32, (size, size), 0)
    c_i = lax.broadcasted_iota(jnp.int32, (size, size), 1)
    perm2[...] = jnp.where(r_i == column_of(c_i), 1.0, 0.0).astype(BF16)
    reorder = one_hot(R, R, lambda r: (r % HALF) * 2 + r // HALF)
    for c in range(CL):
        leaf_perm[c] = nn(reorder, leaf[c]).astype(BF16)

    places = (1, jnp.where(core == 0, 2, 0), jnp.where(core == 0, 0, 2))

    def prepare(s):
        first = pl.multiple_of(places[s] * GSLOTS, GSLOTS)
        x_rows = []
        for j in range(j_count):
            x_rows.append(jnp.concatenate(
                [coup[pl.ds(first + a * t_count, t_count), j * LANES : (j + 1) * LANES]
                 for a in range(a_count)], axis=1))
        xs = jnp.concatenate(x_rows, axis=0)
        ys = nn(perm1[...], xs).astype(BF16)
        ws = nn(ys, perm2[...]).astype(BF16)
        lane_slot = lax.broadcasted_iota(jnp.int32, (1, LANES), 1) // HALF
        for t in range(t_count):
            code = jnp.full((1, LANES), -1, jnp.int32)
            for a in range(a_count):
                b = first + a * t_count + t
                slot_row = jnp.where(live_ref[b] != 0, rows_ref[b], -1)
                code = jnp.where(lane_slot == a, slot_row, code)
            for i in range(CL):
                mask = jnp.where(code == i, 1.0, 0.0)
                mask = jnp.broadcast_to(mask, (j_count, LANES)).astype(BF16)
                for kp in range(2):
                    for h in range(2):
                        tile = ws[t * j_count : (t + 1) * j_count,
                                  (kp * 2 + h) * LANES : (kp * 2 + h + 1) * LANES]
                        lhs[s, (h * CL + i) * R + kp * HALF : (h * CL + i) * R + (kp + 1) * HALF,
                            t * LANES : (t + 1) * LANES] = tile * mask

    def multiply(s, panel):
        first = places[s] * GSLOTS
        x_shift = 3 + ny.bit_length() - 1
        for t in range(t_count):
            for a in range(a_count):
                c = cols_ref[first + a * t_count + t]
                at = (t * a_count + a) * HALF
                gathered[at : at + HALF] = panel[
                    (c >> x_shift) & (nx - 1), (c >> 3) & (ny - 1), c & (2 * CL - 1)
                ]
        part = nn(lhs[s], gathered[...])
        if s == 0:
            acc[...] = part
        else:
            acc[...] += part

    for copy in stage[2:]:
        copy.wait()
    prepare(0)
    pass_on(a1, a2)


    def pair_up():
        then(0, to_opp)

    pl.when(special)(pair_up)
    then(2, to_near)
    to_near.wait_recv()
    begin(n1[0] + n1[1])
    prepare(1)
    pl.when(jnp.logical_not(special))(pair_up)

    def far_step():
        to_opp.wait_recv()
        begin(b1[0] + b1[1])

    @pl.when(special)
    def _():
        to_taker.wait_recv()
        begin(t1[0] + t1[1])
        far_step()

    pass_on(n1, n2)
    now(early_opp, halo_opp)
    now(early_edge, halo_edge)

    pl.when(jnp.logical_not(special))(far_step)

    prepare(2)
    def near_field(c, first, signals):
        wide = jnp.concatenate(signals, axis=1)
        weights = jnp.concatenate([near[c, first + i] for i in range(len(signals))], axis=1)
        return nt(wide, weights)

    for c in range(CL):
        low, high = max(c - 1, 0), min(c + 1, CL - 1)
        total[c] = near_field(c, low - c + 1, [sig[i] for i in range(low, high + 1)])

    start = other_start
    usual = jnp.logical_not(special)
    forwards = jnp.logical_not(late_near)
    pair_low, pair_high = pl.ds(start, 2), pl.ds(start + 2, 2)
    every = slice(None)

    def forward(at):
        copy = prepared(own.at[at], neighbour.at[at], near_z, forwards)
        pl.when(forwards)(copy.start)
        return [copy]

    def share(at):
        return send_all([(own.at[at], sibling.at[at], sib)])

    arrived(a2[0] + a2[1])
    s_all = share((every, every, mine))
    arrived(b1[0])
    line = own.at[x, :, pair_low]
    b2x = send_all([(line, line, dev) for _, dev in x_peers])
    f_low, = forward((x, every, pair_low))
    arrived(b1[1])
    line = own.at[:, y, pair_high]
    b2y = send_all([(line, line, dev) for _, dev in y_peers])
    f_high, = forward((every, y, pair_high))
    pl.when(early_opp)(halo_opp.start)
    then(1, halo_edge)
    s_all += share((x, every, pair_low)) + share((every, y, pair_high))
    m_low = neighbour.at[x, :, pl.ds(next_other, 1)]
    m_high = neighbour.at[:, y, pl.ds(next_other + 2, 1)]
    m2 = (
        [prepared(m_low, m_low, dev, usual) for _, dev in x_peers],
        [prepared(m_high, m_high, dev, usual) for _, dev in y_peers],
    )

    def spread_next():
        pass_on(([f_low], [f_high]), m2)

    pl.when(usual)(spread_next)
    pl.when(special)(functools.partial(pass_on, t1, t2))
    fwd = []
    for i in range(max(nx, ny) - 1):
        if i < nx - 1:
            b2x[i].wait_recv()
            px = (x + nx - ring(nx)[i]) % nx
            s_all += share((px, every, pair_low))
            fwd += forward((px, every, pl.ds(start + 1, 1)))
        if i < ny - 1:
            b2y[i].wait_recv()
            py = (y + ny - ring(ny)[i]) % ny
            s_all += share((every, py, pair_high))
            fwd += forward((every, py, pl.ds(start + 3, 1)))
    def multiply_next():
        arrived(n2[0] + n2[1])
        pl.when(usual)(functools.partial(arrived, m2[0] + m2[1] + fwd))
        pl.when(special)(functools.partial(arrived, t2[0] + t2[1]))
        multiply(2, neighbour)

    multiply(0, own)
    halo_opp.wait_recv()
    halo_edge.wait_recv()
    left = jnp.where(linear == 0, jnp.zeros_like(zero), halo[0])
    right = jnp.where(linear == count - 1, jnp.zeros_like(zero), halo[1])
    total[0] += near_field(0, 0, [left])
    total[CL - 1] += near_field(CL - 1, 2, [right])

    first_plane = jnp.logical_and(plane == 0, z == 0)
    pl.when(first_plane)(multiply_next)
    arrived(s_all)
    multiply(1, sibling)
    pl.when(jnp.logical_not(first_plane))(multiply_next)

    both = acc[0 : CL * R] + pltpu.roll(acc[CL * R :], R, 1)
    far = both[:, 0:R].astype(BF16)
    for c in range(CL):
        part = lax.dot_general(
            far[c * R : (c + 1) * R], leaf_perm[c], (((0,), (0,)), ((), ())),
            preferred_element_type=F32,
        )
        out_ref[c] = (total[c] + part).astype(BF16)
    for copy, when in everything:
        if when is None:
            copy.wait_send()
        else:
            pl.when(when)(copy.wait_send)


def per_device(nx, ny, nz, signal, leaf_basis, near_blocks, coupling, block_cols, block_rows, block_live):
    index = pltpu.SMEM((3 * GSLOTS,), jnp.int32)
    hbm = pl.BlockSpec(memory_space=pltpu.HBM)
    panel = pltpu.VMEM((nx, ny, 2 * CL, HALF, LANES), BF16)
    copies = 96
    return pl.pallas_call(
        functools.partial(kernel, nx, ny, nz),
        name="h2_product",
        out_shape=jax.ShapeDtypeStruct((CL, R, LEAF), BF16),
        in_specs=[hbm] * 7,
        out_specs=pl.BlockSpec(memory_space=pltpu.VMEM),
        scratch_shapes=[
            index, index, index,
            pltpu.VMEM((CL, R, LEAF), BF16),
            pltpu.VMEM((CL, R, LEAF), BF16),
            pltpu.VMEM((CL, 3, LEAF, LEAF), BF16),
            pltpu.VMEM((3 * GSLOTS, R * R), BF16),
            panel, panel, panel,
            pltpu.VMEM((2, R, LEAF), BF16),
            pltpu.VMEM((3, 2 * CL * R, GSLOTS * HALF), BF16),
            pltpu.VMEM((GSLOTS * HALF, LANES), BF16),
            pltpu.VMEM((2 * CL * R, LANES), F32),
            pltpu.VMEM((CL, R, LEAF), F32),
            pltpu.VMEM((512, 512), BF16),
            pltpu.VMEM((512, 512), BF16),
            pltpu.VMEM((CL, R, LEAF), BF16),
            pltpu.SemaphoreType.DMA((7,)),
            pltpu.SemaphoreType.DMA((copies,)),
            pltpu.SemaphoreType.DMA((copies,)),
            pltpu.SemaphoreType.REGULAR((3,)),
        ],
        compiler_params=pltpu.CompilerParams(
            collective_id=0, has_side_effects=True, vmem_limit_bytes=60 * 2**20
        ),
    )(block_cols, block_rows, block_live, signal, leaf_basis, near_blocks, coupling)


def solution(mesh, nx=SIDE, ny=SIDE):
    both = ("grp", "row")
    in_specs = (
        P(both, None, None), P(both, None, None), P(both, None, None, None), P(both, None),
        P(both), P(both), P(both),
    )
    nz = mesh.shape["grp"] // 2
    return jax.shard_map(
        functools.partial(per_device, nx, ny, nz), mesh=mesh, in_specs=in_specs,
        out_specs=P(both, None, None), check_vma=False,
    )
```
